256 devices in a mesh: ctx: 16 (over x, z_lo, core), row: 4 (over y), col: 4 (over z_hi).
Axes of the slice: x: 4, y: 4, z: 8 (z_hi: 4, z_lo: 2; z = z_hi * 2 + z_lo), core: 2. Of those that a mesh axis runs over, the one named last changes fastest.
Arguments:
- activations: bfloat16 [16384, 4096], P('ctx', 'col'), may hold values from -640 to 640
- norm_gain: float32 [4096], P('col'), may hold values from 0.1 to 1.9
- w_query: bfloat16 [4096, 4096], P(('row', 'ctx'), 'col'), may hold values from -0.09375 to 0.09375
- w_key: bfloat16 [4096, 4096], P(('row', 'ctx'), 'col'), may hold values from -0.09375 to 0.09375
- w_value: bfloat16 [4096, 4096], P(('row', 'ctx'), 'col'), may hold values from -0.09375 to 0.09375
- short_taps: float32 [3, 3, 4096], P(None, None, ('row', 'col')), may hold values from -2.5 to 2.5
- long_taps: float32 [128, 4096], P(None, ('row', 'col')), may hold values from -0.5 to 0.5
- skip_gain: float32 [4096], P(('row', 'col')), may hold values from -4 to 4
- w_out: bfloat16 [4096, 4096], P(('col', 'ctx'), 'row'), may hold values from -0.09375 to 0.09375
Outputs:
- mixer_out: bfloat16 [16384, 4096], P(('ctx', 'row'), 'col')
The draws below stay inside these ranges and needn't reach their ends.
All inputs are finite; a program needn't handle non-finite values.
Results may differ from the reference program's by a relative error of at most 0.03.
Values may be sent and summed in bfloat16 or wider, within the bound.
No kernel may reach another device: no remote copies, remote signals or barrier semaphores. Data moves between devices by JAX's collectives and lax.ppermute only.
A program may use at most 128 MiB of HBM per device.

```python
import jax
import jax.numpy as jnp
from jax import lax

D = 4096
C = 4096
SHORT_LEN = 3
FILTER_LEN = 128
TOKENS = 16384
N_ROW = 4
N_COL = 4


def draw_activations(key, part):
    first_key, second_key = jax.random.split(key, 2)
    column_scale = jnp.power(10.0, jnp.arange(D, dtype=jnp.float32) / (D - 1))
    base_vals = jax.random.normal(first_key, (TOKENS, D), jnp.float32)
    row_scale = jnp.exp(jax.random.uniform(second_key, (TOKENS, 1), jnp.float32, 0.0, jnp.log(10.0)))
    base_vals = jnp.clip(base_vals, -4.0, 4.0)
    return (base_vals * column_scale[None, :] * row_scale).astype(jnp.bfloat16)


def level_of(own_key, dims, cuts, low, top_value):
    factor_of, own = 1.0, jax.random.fold_in(own_key, 6)
    for dim, parts in cuts:
        draws = jnp.exp(jax.random.uniform(jax.random.fold_in(own, dim), (parts,), jnp.float32, low / len(cuts), top_value / len(cuts)))
        factor_of = factor_of * jnp.repeat(draws, dims[dim] // parts).reshape([-1 if axis == dim else 1 for axis in range(len(dims))])
    return factor_of


def normal_values(rng, dims, width, most, pieces=(), held_as=jnp.bfloat16):
    level = level_of(rng, dims, pieces, -0.22, 0.18) if pieces else 1.0
    entries = jax.random.normal(rng, dims, jnp.float32) * width * level
    return jnp.minimum(jnp.maximum(entries, -most), most).astype(held_as)


def setup_inputs(seed: int = 0) -> dict:
    splits = jax.random.split(jax.random.key(seed), 10)
    activations = draw_activations(jax.random.fold_in(splits[9], 71), 0)
    norm_gain = jnp.clip(1.0 + 0.18 * jax.random.normal(splits[1], (D,), jnp.float32), 0.1, 1.9)
    w_query = normal_values(splits[2], (C, D), D ** -0.5, 0.09375, ((0, 64), (1, 4)))
    w_key = normal_values(splits[3], (C, D), D ** -0.5, 0.09375, ((0, 64), (1, 4)))
    w_value = normal_values(splits[4], (C, D), D ** -0.5, 0.09375, ((0, 64), (1, 4)))
    short_taps = normal_values(splits[5], (3, SHORT_LEN, C), 0.4, 2.5, ((2, 16),), jnp.float32)
    long_taps = normal_values(splits[6], (FILTER_LEN, C), FILTER_LEN ** -0.5, 0.5, ((1, 16),), jnp.float32)
    skip_gain = normal_values(splits[7], (C,), 1.0, 4.0, ((0, 16),), jnp.float32)
    w_out = normal_values(splits[8], (D, C), C ** -0.5, 0.09375, ((0, 64), (1, 4)))
    return {"activations": activations, "norm_gain": norm_gain, "w_query": w_query, "w_key": w_key, "w_value": w_value, "short_taps": short_taps, "long_taps": long_taps, "skip_gain": skip_gain, "w_out": w_out}


epsilon = 1e-05

def causal_filter(signal, tap_vals):
    tap_count = tap_vals.shape[0]
    kernel = jnp.transpose(jnp.flip(tap_vals, axis=0))[:, None, :]
    result = lax.conv_general_dilated(signal[None], kernel, (1,), [(tap_count - 1, 0)], dimension_numbers=('NCH', 'OIH', 'NCH'), feature_group_count=signal.shape[0], precision=lax.Precision.HIGHEST)
    return result[0]

def reference(activations, norm_gain, w_query, w_key, w_value, short_taps, long_taps, skip_gain, w_out):
    as_float = activations.astype(jnp.float32)
    squares = lax.optimization_barrier(jnp.sum(as_float * as_float, axis=1, keepdims=True))
    normed = (as_float * lax.rsqrt(squares / D + epsilon) * norm_gain).astype(jnp.bfloat16)
    quarter = D // N_COL
    token_count = normed.shape[0]
    group_size = min(C, 256)
    group_count = C // group_size

    def project(weight_rows):
        running = jnp.zeros((weight_rows.shape[0], token_count), jnp.float32)
        for block_idx in range(N_COL):
            part_sum = lax.dot_general(weight_rows[:, block_idx * quarter:(block_idx + 1) * quarter], normed[:, block_idx * quarter:(block_idx + 1) * quarter], (((1,), (1,)), ((), ())), preferred_element_type=jnp.float32)
            running = running + lax.optimization_barrier(part_sum.astype(jnp.bfloat16)).astype(jnp.float32)
        return running.astype(jnp.bfloat16)

    def channel_group(operands):
        query_rows, key_rows, value_rows, short_group, long_group, skip_group = operands
        query_vals = causal_filter(project(query_rows).astype(jnp.float32), short_group[0])
        key_vals = causal_filter(project(key_rows).astype(jnp.float32), short_group[1])
        value_vals = causal_filter(project(value_rows).astype(jnp.float32), short_group[2])
        gate_vals = key_vals * value_vals
        long_part = causal_filter(gate_vals, long_group)
        return (query_vals * (long_part + skip_group[:, None] * gate_vals)).astype(jnp.bfloat16)
    mixed_all = lax.map(channel_group, (w_query.reshape(group_count, group_size, D), w_key.reshape(group_count, group_size, D), w_value.reshape(group_count, group_size, D), jnp.moveaxis(short_taps.reshape(3, SHORT_LEN, group_count, group_size), 2, 0), jnp.moveaxis(long_taps.reshape(FILTER_LEN, group_count, group_size), 1, 0), skip_gain.reshape(group_count, group_size)))
    mixed_all = mixed_all.reshape(C, token_count)
    fourth = C // N_ROW
    running = jnp.zeros((token_count, D), jnp.float32)
    for block_idx in range(N_ROW):
        part_sum = lax.dot_general(mixed_all[block_idx * fourth:(block_idx + 1) * fourth], w_out[:, block_idx * fourth:(block_idx + 1) * fourth], (((0,), (1,)), ((), ())), preferred_element_type=jnp.float32)
        running = running + lax.optimization_barrier(part_sum.astype(jnp.bfloat16)).astype(jnp.float32)
    return running.astype(jnp.bfloat16)
```

```python
import jax
import jax.numpy as jnp
from jax import lax
from jax.experimental import pallas as pl
from jax.experimental.pallas import tpu as pltpu
from jax.sharding import PartitionSpec as P

D = 4096
SHORT_LEN = 3
FILTER_LEN = 128
HALO = 144
Q = 256
CH = 256
F = 1024
epsilon = 1e-05
bf16 = jnp.bfloat16
f32 = jnp.float32


def ring(n, step):
    return [(i, (i + step) % n) for i in range(n)]


def shift(x, axis, step):
    return lax.ppermute(x, axis, ring(4, step))


def gather_ring(x, axis):
    half = x.shape[0] // 2
    before = shift(x, axis, 1)
    after = shift(x, axis, -1)
    far_lo = shift(before[:half], axis, 1)
    far_hi = shift(after[half:], axis, -1)
    return before, after, far_lo, far_hi


def project_kernel(x_ref, gain_ref, w_ref, out_ref, normed_ref):
    @pl.when(pl.program_id(0) == 0)
    def _():
        rows = 32

        @pl.loop(0, Q // rows)
        def _(i):
            at = pl.ds(pl.multiple_of(i * rows, rows), rows)
            x = x_ref[at, :].astype(f32)
            squares = jnp.sum(x * x, axis=1, keepdims=True)
            normed_ref[at, :] = (x * lax.rsqrt(squares / D + epsilon) * gain_ref[...]).astype(bf16)

    out_ref[0] = lax.dot_general(
        normed_ref[...], w_ref[0], (((1,), (1,)), ((), ())), preferred_element_type=f32
    ).astype(bf16)


def project(x, gain, w):
    return pl.pallas_call(
        project_kernel,
        grid=(3,),
        in_specs=[
            pl.BlockSpec((Q, D), lambda i: (0, 0)),
            pl.BlockSpec((1, D), lambda i: (0, 0)),
            pl.BlockSpec((1, CH, D), lambda i: (i, 0, 0)),
        ],
        out_specs=pl.BlockSpec((1, Q, CH), lambda i: (i, 0, 0)),
        out_shape=jax.ShapeDtypeStruct((3, Q, CH), bf16),
        scratch_shapes=[pltpu.VMEM((Q, D), bf16)],
        compiler_params=pltpu.CompilerParams(vmem_limit_bytes=24 << 20),
        cost_estimate=pl.CostEstimate(
            flops=2 * Q * 3 * CH * D, bytes_accessed=2 * (Q * D + 3 * CH * D), transcendentals=0
        ),
        name="project",
    )(x, gain, w)


def mix_kernel(row_ref, p0, p1, p2, p3, halo_ref, taps_ref, out_ref, qkv, gate, shifted):
    row = row_ref[0]
    qkv[:, :HALO, :] = halo_ref[...].astype(f32)
    for s, piece in enumerate((p0, p1, p2, p3)):
        start = HALO + lax.rem(row + s, 4) * Q
        for proj in range(3):
            qkv[proj, pl.ds(pl.multiple_of(start, 16), Q), :] = piece[proj].astype(f32)

    step = 64
    for lanes in (pl.ds(0, 128), pl.ds(128, 128)):

        @pl.loop(0, 1152 // step)
        def _(i):
            base = pl.multiple_of(i * step, step) + (HALO - 128)
            total = []
            for proj in (1, 2):
                window = qkv[proj, pl.ds(pl.multiple_of(base - 8, 8), step + 8), lanes]
                acc = None
                for tap in range(SHORT_LEN):
                    term = taps_ref[pl.ds(3 * proj + tap, 1), lanes] * window[8 - tap : 8 - tap + step]
                    acc = term if acc is None else acc + term
                total.append(acc)
            gate[pl.ds(pl.multiple_of(i * step, step), step), lanes] = total[0] * total[1]

        @pl.loop(0, 1144 // 88)
        def _(i):
            base = pl.multiple_of(i * 88, 8)
            window = gate[pl.ds(base, 96), lanes]
            for r in range(8):
                shifted[r, pl.ds(base + 8, 88), lanes] = window[8 - r : 96 - r]

        @pl.loop(0, 8)
        def _(i):
            base = pl.multiple_of(i * 128, 128)
            acc = taps_ref[pl.ds(137, 1), lanes] * gate[pl.ds(base + 128, 128), lanes]
            for j in range(FILTER_LEN):
                acc = acc + taps_ref[pl.ds(9 + j, 1), lanes] * shifted[
                    j % 8, pl.ds(base + 128 - 8 * (j // 8), 128), lanes
                ]
            window = qkv[0, pl.ds(base + HALO - 8, 136), lanes]
            query = None
            for tap in range(SHORT_LEN):
                term = taps_ref[pl.ds(tap, 1), lanes] * window[8 - tap : 136 - tap]
                query = term if query is None else query + term
            place = lax.rem(i // 2 - row + 4, 4) * Q + lax.rem(i, 2) * 128
            out_ref[pl.ds(pl.multiple_of(place, 128), 128), lanes] = (query * acc).astype(bf16)


def mix(row, pieces, halo, taps):
    return pl.pallas_call(
        mix_kernel,
        in_specs=[pl.BlockSpec(memory_space=pltpu.SMEM)] + [pl.BlockSpec(memory_space=pltpu.VMEM)] * 6,
        out_specs=pl.BlockSpec(memory_space=pltpu.VMEM),
        out_shape=jax.ShapeDtypeStruct((4 * Q, CH), bf16),
        scratch_shapes=[
            pltpu.VMEM((3, HALO + 4 * Q, CH), f32),
            pltpu.VMEM((1152, CH), f32),
            pltpu.VMEM((8, 1152, CH), f32),
        ],
        compiler_params=pltpu.CompilerParams(vmem_limit_bytes=32 << 20),
        cost_estimate=pl.CostEstimate(
            flops=2 * 4 * Q * CH * FILTER_LEN * 20, bytes_accessed=4 << 20, transcendentals=0
        ),
        name="mix",
    )(row, *pieces, halo, taps)


def on_device(
    activations, norm_gain, w_query, w_key, w_value, short_taps, long_taps, skip_gain, w_out
):
    row = lax.axis_index("row")
    col = lax.axis_index("col")
    order = jnp.stack([col, (col + 3) % 4, (col + 1) % 4, (col + 2) % 4])

    mine = lax.dynamic_slice_in_dim(activations, row * Q, Q, 0)
    before, after, far_lo, far_hi = gather_ring(mine, "col")

    stacked = jnp.stack([w_query, w_key, w_value]).reshape(3, 4, 16, F)

    def group(i):
        return lax.dynamic_index_in_dim(stacked, i, 1, keepdims=False)

    w_rows = jnp.concatenate(
        [
            group(order[0]),
            shift(group(order[2]), "col", 1),
            shift(group(order[1]), "col", -1),
            shift(group(order[3]), "col", 2),
        ],
        axis=2,
    )
    w_all = lax.all_gather(w_rows, "ctx", axis=1, tiled=True)

    small = jnp.concatenate(
        [short_taps.reshape(9, CH), long_taps, skip_gain[None], norm_gain.reshape(4, CH)], axis=0
    )
    small_all = lax.all_gather(small, "col", axis=0, tiled=False)
    gain = jnp.take(small_all[:, 138:].reshape(4, F), order, axis=0).reshape(1, D)
    n = jnp.arange(CH)
    wanted = (n // 16) * 64 + col * 16 + n % 16
    pick = (jnp.arange(F)[:, None] == wanted[None, :]).astype(f32)
    taps = jnp.dot(
        jnp.transpose(small_all[:, :138], (1, 0, 2)).reshape(138, F), pick, precision=lax.Precision.HIGHEST
    )

    full = jnp.concatenate([mine, before, after, jnp.concatenate([far_lo, far_hi], 0)], axis=1)
    y_before, y_after, y_far_lo, y_far_hi = gather_ring(full, "row")
    y_far = jnp.concatenate([y_far_lo, y_far_hi], 0)
    pieces = [project(x, gain, w_all) for x in (full, y_after, y_far, y_before)]

    tails = jnp.stack([piece[:, Q - HALO :] for piece in pieces])
    tail = lax.dynamic_index_in_dim(tails, (3 - row) % 4, 0, keepdims=False)
    halo = lax.ppermute(tail, "ctx", [(i, i + 1) for i in range(15)])

    mixed = mix(row[None], pieces, halo, taps)

    m = jnp.arange(F)
    blocks = order[m // 256]
    wanted_out = ((m % 256) // 16) * 64 + blocks * 16 + m % 16
    pick_out = (jnp.arange(F)[:, None] == wanted_out[None, :]).astype(bf16)
    out_rows = jnp.dot(w_out, pick_out, preferred_element_type=f32).astype(bf16)
    out_all = lax.all_gather(out_rows, "ctx", axis=0, tiled=True)

    m_before, m_after, m_far_lo, m_far_hi = gather_ring(mixed, "col")
    mixed_all = jnp.concatenate(
        [mixed, m_before, m_after, jnp.concatenate([m_far_lo, m_far_hi], 0)], axis=1
    )
    part = lax.dot_general(
        mixed_all, out_all, (((1,), (1,)), ((), ())), preferred_element_type=f32
    ).astype(bf16)
    part = part.reshape(4, Q, F)
    got = [part[0], shift(part[1], "row", 1), shift(part[2], "row", 2), shift(part[3], "row", -1)]
    return sum(g.astype(f32) for g in got).astype(bf16)


def solution(mesh):
    in_specs = (
        P("ctx", "col"),
        P("col"),
        P(("row", "ctx"), "col"),
        P(("row", "ctx"), "col"),
        P(("row", "ctx"), "col"),
        P(None, None, ("row", "col")),
        P(None, ("row", "col")),
        P(("row", "col")),
        P(("col", "ctx"), "row"),
    )
    out_specs = P(("ctx", "row"), "col")
    return jax.shard_map(
        on_device, mesh=mesh, in_specs=in_specs, out_specs=out_specs, check_vma=False
    )
```

```python
import functools

import jax
import jax.numpy as jnp
from jax import lax
from jax.experimental import pallas as pl
from jax.experimental.pallas import tpu as pltpu
from jax.sharding import PartitionSpec as P

D = 4096
SHORT_LEN = 3
FILTER_LEN = 128
HALO = 144
Q = 256
CH = 256
F = 1024
epsilon = 1e-05
bf16 = jnp.bfloat16
f32 = jnp.float32


def ring(n, step):
    return [(i, (i + step) % n) for i in range(n)]


def shift(x, axis, step):
    return lax.ppermute(x, axis, ring(4, step))


def project_kernel(count, *refs):
    pieces, w_hbm, out_ref, x, w, scale_ref, x_sems, w_sems = refs[: 4 * count], *refs[4 * count :]
    x_copies = [pltpu.make_async_copy(piece, x.at[i], x_sems.at[i]) for i, piece in enumerate(pieces)]
    w_copies = [pltpu.make_async_copy(w_hbm.at[i], w.at[i], w_sems.at[i]) for i in range(16)]
    for copy in x_copies + w_copies:
        copy.start()
    rows = 64
    for s in range(count):
        for copy in x_copies[4 * s : 4 * s + 4]:
            copy.wait()

    @pl.loop(0, count * (Q // rows))
    def _(i):
        s = i // (Q // rows)
        at = pl.ds(pl.multiple_of(lax.rem(i, Q // rows) * rows, rows), rows)
        squares = None
        for b in range(4):
            values = x[4 * s + b, at, :].astype(f32)
            part = jnp.sum(values * values, axis=1, keepdims=True)
            squares = part if squares is None else squares + part
        scale_ref[s, at, :] = jnp.broadcast_to(lax.rsqrt(squares / D + epsilon), (rows, 128))

    for copy in w_copies:
        copy.wait()

    @pl.loop(0, 3 * count)
    def _(i):
        p, s = i // count, lax.rem(i, count)
        total = None
        for b in range(4):
            part = lax.dot_general(
                x[4 * s + b],
                w[:, p, :, F * b : F * b + F].reshape(CH, F),
                (((1,), (1,)), ((), ())),
                preferred_element_type=f32,
            )
            total = part if total is None else total + part
        scale = scale_ref[s]
        for lanes in (slice(0, 128), slice(128, 256)):
            out_ref[p, pl.ds(pl.multiple_of(s * Q, Q), Q), lanes] = (total[:, lanes] * scale).astype(bf16)


def project(pieces, w):
    count = len(pieces) // 4
    anywhere = pl.BlockSpec(memory_space=pl.ANY)
    return pl.pallas_call(
        functools.partial(project_kernel, count),
        in_specs=[anywhere] * (4 * count + 1),
        out_specs=pl.BlockSpec(memory_space=pltpu.VMEM),
        out_shape=jax.ShapeDtypeStruct((3, count * Q, CH), bf16),
        scratch_shapes=[
            pltpu.VMEM((4 * count, Q, F), bf16),
            pltpu.VMEM((16, 3, 16, D), bf16),
            pltpu.VMEM((count, Q, 128), f32),
            pltpu.SemaphoreType.DMA((4 * count,)),
            pltpu.SemaphoreType.DMA((16,)),
        ],
        compiler_params=pltpu.CompilerParams(vmem_limit_bytes=56 << 20),
        cost_estimate=pl.CostEstimate(
            flops=2 * count * Q * 3 * CH * D,
            bytes_accessed=2 * (count * Q * D + 3 * CH * D),
            transcendentals=0,
        ),
        name="project",
    )(*pieces, w)


HALF = 512


def mix_kernel(first, row_ref, near_ref, far_ref, halo_ref, taps_ref, out_ref, qkv, gate, shifted):
    row = row_ref[0]
    if first:
        qkv[:, :HALO, :] = halo_ref[...].astype(f32)
    for s, (ref, at) in enumerate(((near_ref, 0), (near_ref, Q), (far_ref, 0), (near_ref, 2 * Q))):
        start = pl.multiple_of(lax.rem(row + s, 4) * Q + HALO, 16)
        for proj in range(3):
            qkv[proj, pl.ds(start, Q), :] = ref[proj, at : at + Q, :].astype(f32)
    offset = 0 if first else HALF

    step = 64

    @pl.loop(0, 2)
    def _(lane_block):
        lanes = pl.ds(pl.multiple_of(lane_block * 128, 128), 128)

        @pl.loop(0, (HALF + 128) // step)
        def _(i):
            base = pl.multiple_of(i * step, step) + (HALO - 128 + offset)
            total = []
            for proj in (1, 2):
                window = qkv[proj, pl.ds(pl.multiple_of(base - 8, 8), step + 8), lanes]
                acc = None
                for tap in range(SHORT_LEN):
                    term = taps_ref[pl.ds(3 * proj + tap, 1), lanes] * window[8 - tap : 8 - tap + step]
                    acc = term if acc is None else acc + term
                total.append(acc)
            gate[pl.ds(pl.multiple_of(i * step, step) + 8, step), lanes] = total[0] * total[1]

        @pl.loop(0, (HALF + 128) // 64)
        def _(i):
            base = pl.multiple_of(i * 64, 64)
            window = gate[pl.ds(base, 72), lanes]
            for r in range(8):
                shifted[r, pl.ds(base, 64), lanes] = window[8 - r : 72 - r]

        @pl.loop(0, HALF // 128)
        def _(i):
            base = pl.multiple_of(i * 128, 128)
            acc = taps_ref[pl.ds(137, 1), lanes] * gate[pl.ds(base + 136, 128), lanes]
            for r in range(8):
                window = shifted[r, pl.ds(base + 8, 248), lanes]
                for m in range(16):
                    acc = acc + taps_ref[pl.ds(9 + 8 * m + r, 1), lanes] * window[120 - 8 * m : 248 - 8 * m]
            window = qkv[0, pl.ds(base + (HALO - 8 + offset), 136), lanes]
            query = None
            for tap in range(SHORT_LEN):
                term = taps_ref[pl.ds(tap, 1), lanes] * window[8 - tap : 136 - tap]
                query = term if query is None else query + term
            out_ref[pl.ds(base, 128), lanes] = (query * acc).astype(bf16)


def mix(first, row, near, far, halo, taps):
    return pl.pallas_call(
        functools.partial(mix_kernel, first),
        in_specs=[pl.BlockSpec(memory_space=pltpu.SMEM)] + [pl.BlockSpec(memory_space=pltpu.VMEM)] * 4,
        out_specs=pl.BlockSpec(memory_space=pltpu.VMEM),
        out_shape=jax.ShapeDtypeStruct((HALF, CH), bf16),
        scratch_shapes=[
            pltpu.VMEM((3, HALO + 4 * Q, CH), f32),
            pltpu.VMEM((HALF + 136, CH), f32),
            pltpu.VMEM((8, HALF + 128, CH), f32),
        ],
        compiler_params=pltpu.CompilerParams(vmem_limit_bytes=24 << 20),
        cost_estimate=pl.CostEstimate(
            flops=9_000_000_000, bytes_accessed=2 << 20, transcendentals=0
        ),
        name="mix",
    )(row, near, far, halo, taps)


def shard_of(n):
    return n // 4 * 4 + n % 2 * 2 + n // 2 % 2


def after(x, *others):
    return lax.optimization_barrier((x, others))[0]


def gather_col(x):
    half = x.shape[0] // 2
    before = shift(x, "col", 1)
    behind = shift(x, "col", -1)
    far = [shift(before[:half], "col", 1), shift(behind[half:], "col", -1)]
    return [x, before, behind, jnp.concatenate(far, 0)]


HF = F // 2


def on_device(
    activations, norm_gain, w_query, w_key, w_value, short_taps, long_taps, skip_gain, w_out
):
    row = lax.axis_index("row")
    col = lax.axis_index("col")
    order = jnp.stack([col, (col + 3) % 4, (col + 1) % 4, (col + 2) % 4])

    stacked = (jnp.stack([w_query, w_key, w_value]).astype(f32) * norm_gain).astype(bf16).reshape(3, 4, 16, F)

    def group(i):
        return lax.dynamic_index_in_dim(stacked, i, 1, keepdims=False).reshape(48, F)

    own = lax.dynamic_slice_in_dim(activations, row * Q, Q, 0)

    def payload(x, w):
        return jnp.concatenate([x, w[:, :HF], w[:, HF:]], axis=0)

    own_from_before = shift(own, "row", 1)
    own_from_after = shift(own, "row", -1)
    up = shift(payload(own[:, :HF], group(order[2])), "col", 1)
    down = shift(payload(own[:, HF:], group(order[1])), "col", -1)
    w_far = shift(group(order[3]), "col", 2)
    w_up = (up[Q : Q + 48], up[Q + 48 :])
    w_down = (down[Q : Q + 48], down[Q + 48 :])
    w_rows = jnp.concatenate(
        [group(order[0]), w_up[0], w_down[1], w_down[0], w_up[1], w_far], axis=1
    )
    w_rows = after(w_rows, own_from_before, own_from_after)
    low_z = (lax.axis_index("ctx") // 2) % 2 == 0
    w_other = lax.ppermute(w_rows, "ctx", [(i, i ^ 2) for i in range(16)])

    mixed_up = jnp.concatenate([up[:Q], down[:Q]], axis=1)
    up_from_before = shift(mixed_up, "row", 1)
    up_from_after = shift(mixed_up, "row", -1)

    w_pair = jnp.concatenate([jnp.where(low_z, w_rows, w_other), jnp.where(low_z, w_other, w_rows)], axis=0)
    rest_up = shift(own[:, HF:], "col", 1)
    rest_down = shift(own[:, :HF], "col", -1)
    far_own = shift(own_from_before, "row", 1)
    w_pair = after(w_pair, up_from_before, up_from_after, rest_up, rest_down, far_own)
    groups = [[4 * x + 2 * z + core for x in range(4) for core in range(2)] for z in range(2)]
    w_all = lax.all_gather(w_pair, "ctx", axis=0, tiled=True, axis_index_groups=groups).reshape(16, 3, 16, D)

    far_up = shift(up[:Q], "col", 1)
    far_down = shift(down[:Q], "col", -1)
    own = [
        own,
        mixed_up,
        jnp.concatenate([rest_down, rest_up], axis=1),
        jnp.concatenate([far_up, far_down], axis=1),
    ]
    from_before = [own_from_before, up_from_before] + [shift(x, "row", 1) for x in own[2:]]
    from_after = [own_from_after, up_from_after] + [shift(x, "row", -1) for x in own[2:]]
    far = [far_own, shift(up_from_before, "row", 1)] + [shift(x, "row", -1) for x in from_after[2:]]
    near_out = project(own + from_after + from_before, w_all)
    far_out = project([after(far[0], near_out)] + far[1:], w_all)

    small = jnp.concatenate(
        [short_taps.reshape(9, CH), long_taps, skip_gain[None], jnp.zeros((6, CH), f32)], axis=0
    )
    small = after(small, far_up, far_down)
    v = jnp.arange(512)
    wanted = shard_of(v % 128 // 16) * 64 + order[v // 128] * 16 + v % 16
    pick = ((jnp.arange(CH)[:, None] == wanted[None, :]) & (v % 128 < 64)[None, :]).astype(f32)
    small = jnp.dot(small, pick, precision=lax.Precision.HIGHEST)
    small = jnp.concatenate(
        [
            small[:, :128],
            shift(small[:, 256:384], "col", 1),
            shift(small[:, 128:256], "col", -1),
            shift(small[:, 384:], "col", 2),
        ],
        axis=1,
    )
    place = ((order[v // 128] * 64 + v % 128)[:, None] == jnp.arange(CH)[None, :]) & (v % 128 < 64)[:, None]
    taps = jnp.dot(small, place.astype(f32), precision=lax.Precision.HIGHEST)

    m = jnp.arange(F)
    blocks = order[m // 256]
    wanted_out = shard_of((m % 256) // 16) * 64 + blocks * 16 + m % 16
    pick_out = (jnp.arange(F)[:, None] == wanted_out[None, :]).astype(bf16)
    out_rows = jnp.dot(w_out, pick_out, preferred_element_type=f32).astype(bf16)
    out_all = lax.all_gather(out_rows, "ctx", axis=0, tiled=True)

    tails = [near_out[:, Q - HALO : Q], near_out[:, 2 * Q - HALO : 2 * Q], far_out[:, Q - HALO :], near_out[:, 3 * Q - HALO :]]
    tail = lax.dynamic_index_in_dim(jnp.stack(tails), (3 - row) % 4, 0, keepdims=False)
    halo = lax.ppermute(tail, "ctx", [(i, i + 1) for i in range(15)])

    late = mix(False, row[None], near_out, far_out, tail, taps)
    early = mix(True, row[None], near_out, far_out, halo, taps)
    mixed = jnp.concatenate([early, late], axis=0).reshape(4, Q, CH)

    def quarter(s):
        return lax.dynamic_index_in_dim(mixed, (row + s) % 4, 0, keepdims=False)

    first = gather_col(jnp.concatenate([quarter(2), quarter(1)], axis=0))
    second = gather_col(after(jnp.concatenate([quarter(3), quarter(0)], axis=0), first[1], first[2]))

    def outputs(gathered):
        return lax.dot_general(
            jnp.concatenate(gathered, axis=1), out_all, (((1,), (1,)), ((), ())), preferred_element_type=f32
        ).astype(bf16)

    part = outputs(first)
    got = [shift(part[:Q], "row", 2), shift(part[Q:], "row", 1)]
    part = outputs(second)
    got += [shift(part[:Q], "row", -1), part[Q:]]
    return sum(g.astype(f32) for g in got).astype(bf16)


def solution(mesh):
    in_specs = (
        P("ctx", "col"),
        P("col"),
        P(("row", "ctx"), "col"),
        P(("row", "ctx"), "col"),
        P(("row", "ctx"), "col"),
        P(None, None, ("row", "col")),
        P(None, ("row", "col")),
        P(("row", "col")),
        P(("col", "ctx"), "row"),
    )
    out_specs = P(("ctx", "row"), "col")
    return jax.shard_map(
        on_device, mesh=mesh, in_specs=in_specs, out_specs=out_specs, check_vma=False
    )
```

```python
import functools

import jax
import jax.numpy as jnp
from jax import lax
from jax.experimental import pallas as pl
from jax.experimental.pallas import tpu as pltpu
from jax.sharding import PartitionSpec as P

D = 4096
SHORT_LEN = 3
FILTER_LEN = 128
HALO = 144
Q = 256
CH = 256
F = 1024
epsilon = 1e-05
bf16 = jnp.bfloat16
f32 = jnp.float32


def ring(n, step):
    return [(i, (i + step) % n) for i in range(n)]


def shift(x, axis, step):
    return lax.ppermute(x, axis, ring(4, step))


TOKENS = 4 * Q


def project_kernel(quarters, row_ref, act_hbm, *refs):
    count = len(quarters)
    pieces, w_hbm, out_ref, x, w, scale_ref, x_sems, w_sems = refs[: 3 * count], *refs[3 * count :]
    row = row_ref[0]
    x_copies = []
    for s, quarter in enumerate(quarters):
        own = pl.ds(pl.multiple_of(lax.rem(row + quarter, 4) * Q, Q), Q)
        for b, source in enumerate([act_hbm.at[own, :], *pieces[3 * s : 3 * s + 3]]):
            x_copies.append(
                pltpu.make_async_copy(source, x.at[pl.ds(Q * s, Q), pl.ds(F * b, F)], x_sems.at[4 * s + b])
            )

    def w_copies(p):
        return [
            pltpu.make_async_copy(w_hbm.at[i, p], w.at[p, pl.ds(16 * i, 16), :], w_sems.at[p, i]) for i in range(16)
        ]

    for copy in x_copies + w_copies(0) + w_copies(1) + w_copies(2):
        copy.start()
    rows = 64
    for s in range(count):
        for copy in x_copies[4 * s : 4 * s + 4]:
            copy.wait()

        @pl.loop(Q * s // rows, Q * (s + 1) // rows)
        def _(i):
            at = pl.ds(pl.multiple_of(i * rows, rows), rows)
            squares = None
            for b in range(4):
                values = x[at, F * b : F * b + F].astype(f32)
                part = jnp.sum(values * values, axis=1, keepdims=True)
                squares = part if squares is None else squares + part
            scale_ref[at, :] = jnp.broadcast_to(lax.rsqrt(squares / D + epsilon), (rows, 128))

    @pl.loop(0, 3)
    def _(p):
        for copy in w_copies(p):
            copy.wait()
        total = lax.dot_general(x[...], w[p], (((1,), (1,)), ((), ())), preferred_element_type=f32)
        scale = scale_ref[...]
        for lanes in (slice(0, 128), slice(128, 256)):
            out_ref[p, :, lanes] = (total[:, lanes] * scale).astype(bf16)


def project(row, quarters, activations, pieces, w):
    count = len(quarters)
    anywhere = pl.BlockSpec(memory_space=pl.ANY)
    return pl.pallas_call(
        functools.partial(project_kernel, quarters),
        in_specs=[pl.BlockSpec(memory_space=pltpu.SMEM)] + [anywhere] * (3 * count + 2),
        out_specs=pl.BlockSpec(memory_space=pltpu.VMEM),
        out_shape=jax.ShapeDtypeStruct((3, count * Q, CH), bf16),
        scratch_shapes=[
            pltpu.VMEM((count * Q, D), bf16),
            pltpu.VMEM((3, CH, D), bf16),
            pltpu.VMEM((count * Q, 128), f32),
            pltpu.SemaphoreType.DMA((4 * count,)),
            pltpu.SemaphoreType.DMA((3, 16)),
        ],
        compiler_params=pltpu.CompilerParams(vmem_limit_bytes=56 << 20),
        cost_estimate=pl.CostEstimate(
            flops=4_000_000_000 * count, bytes_accessed=2 * (count * Q * D + 3 * CH * D), transcendentals=0
        ),
        name="project",
    )(row, activations, *pieces, w)


HALF = 512


def mix_kernel(first, row_ref, near_ref, far_ref, halo_ref, taps_ref, out_ref, qkv, gate, shifted):
    row = row_ref[0]
    if first:
        qkv[:, :HALO, :] = halo_ref[...].astype(f32)
    for s, (ref, at) in enumerate(((near_ref, 0), (near_ref, Q), (far_ref, 0), (near_ref, 2 * Q))):
        start = pl.multiple_of(lax.rem(row + s, 4) * Q + HALO, 16)
        for proj in range(3):
            qkv[proj, pl.ds(start, Q), :] = ref[proj, at : at + Q, :].astype(f32)
    offset = 0 if first else HALF

    step = 64

    @pl.loop(0, 2)
    def _(lane_block):
        lanes = pl.ds(pl.multiple_of(lane_block * 128, 128), 128)

        @pl.loop(0, (HALF + 128) // step)
        def _(i):
            base = pl.multiple_of(i * step, step) + (HALO - 128 + offset)
            total = []
            for proj in (1, 2):
                window = qkv[proj, pl.ds(pl.multiple_of(base - 8, 8), step + 8), lanes]
                acc = None
                for tap in range(SHORT_LEN):
                    term = taps_ref[pl.ds(3 * proj + tap, 1), lanes] * window[8 - tap : 8 - tap + step]
                    acc = term if acc is None else acc + term
                total.append(acc)
            gate[pl.ds(pl.multiple_of(i * step, step) + 8, step), lanes] = total[0] * total[1]

        @pl.loop(0, (HALF + 128) // 64)
        def _(i):
            base = pl.multiple_of(i * 64, 64)
            window = gate[pl.ds(base, 72), lanes]
            for r in range(8):
                shifted[r, pl.ds(base, 64), lanes] = window[8 - r : 72 - r]

        @pl.loop(0, HALF // 128)
        def _(i):
            base = pl.multiple_of(i * 128, 128)
            acc = taps_ref[pl.ds(137, 1), lanes] * gate[pl.ds(base + 136, 128), lanes]
            for r in range(8):
                window = shifted[r, pl.ds(base + 8, 248), lanes]
                for m in range(16):
                    acc = acc + taps_ref[pl.ds(9 + 8 * m + r, 1), lanes] * window[120 - 8 * m : 248 - 8 * m]
            window = qkv[0, pl.ds(base + (HALO - 8 + offset), 136), lanes]
            query = None
            for tap in range(SHORT_LEN):
                term = taps_ref[pl.ds(tap, 1), lanes] * window[8 - tap : 136 - tap]
                query = term if query is None else query + term
            out_ref[pl.ds(base, 128), lanes] = (query * acc).astype(bf16)


def mix(first, row, near, far, halo, taps):
    return pl.pallas_call(
        functools.partial(mix_kernel, first),
        in_specs=[pl.BlockSpec(memory_space=pltpu.SMEM)] + [pl.BlockSpec(memory_space=pltpu.VMEM)] * 4,
        out_specs=pl.BlockSpec(memory_space=pltpu.VMEM),
        out_shape=jax.ShapeDtypeStruct((HALF, CH), bf16),
        scratch_shapes=[
            pltpu.VMEM((3, HALO + 4 * Q, CH), f32),
            pltpu.VMEM((HALF + 136, CH), f32),
            pltpu.VMEM((8, HALF + 128, CH), f32),
        ],
        compiler_params=pltpu.CompilerParams(vmem_limit_bytes=24 << 20),
        cost_estimate=pl.CostEstimate(
            flops=9_000_000_000, bytes_accessed=2 << 20, transcendentals=0
        ),
        name="mix",
    )(row, near, far, halo, taps)


def shard_of(n):
    return n // 4 * 4 + n % 2 * 2 + n // 2 % 2


def after(x, *others):
    return lax.optimization_barrier((x, others))[0]


def gather_col(x):
    half = x.shape[0] // 2
    before = shift(x, "col", 1)
    behind = shift(x, "col", -1)
    far = [shift(before[:half], "col", 1), shift(behind[half:], "col", -1)]
    return [x, before, behind, jnp.concatenate(far, 0)]


HF = F // 2


def on_device(
    activations, norm_gain, w_query, w_key, w_value, short_taps, long_taps, skip_gain, w_out
):
    row = lax.axis_index("row")
    col = lax.axis_index("col")
    order = jnp.stack([col, (col + 3) % 4, (col + 1) % 4, (col + 2) % 4])

    stacked = (jnp.stack([w_query, w_key, w_value]).astype(f32) * norm_gain).astype(bf16).reshape(3, 4, 16, F)

    def group(i):
        return lax.dynamic_index_in_dim(stacked, i, 1, keepdims=False).reshape(48, F)

    own = lax.dynamic_slice_in_dim(activations, row * Q, Q, 0)

    def payload(x, w):
        return jnp.concatenate([x, w[:, :HF], w[:, HF:]], axis=0)

    up = shift(payload(own[:, :HF], group(order[2])), "col", 1)
    down = shift(payload(own[:, HF:], group(order[1])), "col", -1)
    w_far = shift(group(order[3]), "col", 2)
    w_rows = jnp.concatenate(
        [group(order[0]), up[Q : Q + 48], down[Q + 48 :], down[Q : Q + 48], up[Q + 48 :], w_far], axis=1
    )
    up, down = up[:Q], down[:Q]
    low_z = (lax.axis_index("ctx") // 2) % 2 == 0
    w_other = lax.ppermute(w_rows, "ctx", [(i, i ^ 2) for i in range(16)])
    w_pair = jnp.concatenate([jnp.where(low_z, w_rows, w_other), jnp.where(low_z, w_other, w_rows)], axis=0)
    mixed_up = jnp.concatenate([up, down], axis=1)
    up_from_before = shift(mixed_up, "row", 1)
    up_from_after = shift(mixed_up, "row", -1)
    rest = after(own, up, down)
    rest_up = shift(rest[:, HF:], "col", 1)
    rest_down = shift(rest[:, :HF], "col", -1)
    w_pair = after(w_pair, up_from_before, up_from_after, rest_up, rest_down)
    groups = [[4 * x + 2 * z + core for x in range(4) for core in range(2)] for z in range(2)]
    w_all = lax.all_gather(w_pair, "ctx", axis=0, tiled=True, axis_index_groups=groups).reshape(16, 3, 16, D)

    mixed_rest = jnp.concatenate([rest_down, rest_up], axis=1)
    up, down = after((up, down), rest_up, rest_down)
    far_up = shift(up, "col", 1)
    far_down = shift(down, "col", -1)
    from_before = [up_from_before, shift(mixed_rest, "row", 1)]
    from_after = [up_from_after, shift(mixed_rest, "row", -1)]
    mixed_far = after(jnp.concatenate([far_up, far_down], axis=1), from_before[1], from_after[1])
    from_before.append(shift(mixed_far, "row", 1))
    from_after.append(shift(mixed_far, "row", -1))
    own = [mixed_up, mixed_rest, mixed_far]
    far = [shift(from_before[0], "row", 1), shift(from_after[1], "row", -1)]
    far += [shift(from_before[2][:, :HF], "row", 1), shift(from_after[2][:, HF:], "row", -1)]
    near_out = project(row[None], (0, 1, 3), activations, own + from_after + from_before, w_all)
    small = jnp.concatenate(
        [short_taps.reshape(9, CH), long_taps, skip_gain[None], jnp.zeros((6, CH), f32)], axis=0
    )
    small = after(small, mixed_far)
    v = jnp.arange(512)
    wanted = shard_of(v % 128 // 16) * 64 + order[v // 128] * 16 + v % 16
    pick = ((jnp.arange(CH)[:, None] == wanted[None, :]) & (v % 128 < 64)[None, :]).astype(f32)
    small = jnp.dot(small, pick, precision=lax.Precision.HIGHEST)
    small = [
        small[:, :128],
        shift(small[:, 256:384], "col", 1),
        shift(small[:, 128:256], "col", -1),
        shift(small[:, 384:], "col", 2),
    ]
    far = after(far, near_out)
    far = far[:2] + [jnp.concatenate(far[2:], axis=1)]
    far_out = project(row[None], (2,), activations, far, w_all)

    small = after(small, near_out)
    place = ((order[v // 128] * 64 + v % 128)[:, None] == jnp.arange(CH)[None, :]) & (v % 128 < 64)[:, None]
    taps = jnp.dot(jnp.concatenate(small, axis=1), place.astype(f32), precision=lax.Precision.HIGHEST)

    m = jnp.arange(F)
    blocks = order[m // 256]
    wanted_out = shard_of((m % 256) // 16) * 64 + blocks * 16 + m % 16
    pick_out = (jnp.arange(F)[:, None] == wanted_out[None, :]).astype(bf16)
    w_out = after(w_out, from_before[2])
    out_rows = jnp.dot(w_out, pick_out, preferred_element_type=f32).astype(bf16)
    out_all = lax.all_gather(out_rows, "ctx", axis=0, tiled=True)

    tails = [near_out[:, Q - HALO : Q], near_out[:, 2 * Q - HALO : 2 * Q], far_out[:, Q - HALO :], near_out[:, 3 * Q - HALO :]]
    tail = lax.dynamic_index_in_dim(jnp.stack(tails), (3 - row) % 4, 0, keepdims=False)
    halo = lax.ppermute(tail, "ctx", [(i, i + 1) for i in range(15)])

    late = mix(False, row[None], near_out, far_out, tail, taps)
    early = mix(True, row[None], near_out, far_out, halo, taps)
    mixed = jnp.concatenate([early, late], axis=0).reshape(4, Q, CH)

    def quarter(s):
        return lax.dynamic_index_in_dim(mixed, (row + s) % 4, 0, keepdims=False)

    mid = Q // 2
    opposite, above, below = quarter(2), quarter(1), quarter(3)
    first = gather_col(jnp.concatenate([opposite, above[:mid], below[mid:]], axis=0))
    second = jnp.concatenate([above[mid:], below[:mid], quarter(0)], axis=0)
    second = gather_col(after(second, first[1], first[2]))

    def outputs(gathered):
        return lax.dot_general(
            jnp.concatenate(gathered, axis=1), out_all, (((1,), (1,)), ((), ())), preferred_element_type=f32
        ).astype(bf16)

    def add(a, b):
        return (a.astype(f32) + b.astype(f32)).astype(bf16)

    part = outputs(first)
    opposite_lo = shift(part[:mid], "row", 1)
    opposite_hi = shift(part[mid:Q], "row", -1)
    up_lo = shift(add(part[Q : Q + mid], opposite_lo), "row", 1)
    down_hi = shift(add(part[Q + mid :], opposite_hi), "row", -1)
    part = outputs(second)
    up_hi = shift(part[:mid], "row", 1)
    down_lo = shift(part[mid:Q], "row", -1)
    up = jnp.concatenate([up_lo, up_hi], axis=0)
    down = jnp.concatenate([down_lo, down_hi], axis=0)
    return (part[Q:].astype(f32) + up.astype(f32) + down.astype(f32)).astype(bf16)


def solution(mesh):
    in_specs = (
        P("ctx", "col"),
        P("col"),
        P(("row", "ctx"), "col"),
        P(("row", "ctx"), "col"),
        P(("row", "ctx"), "col"),
        P(None, None, ("row", "col")),
        P(None, ("row", "col")),
        P(("row", "col")),
        P(("col", "ctx"), "row"),
    )
    out_specs = P(("ctx", "row"), "col")
    return jax.shard_map(
        on_device, mesh=mesh, in_specs=in_specs, out_specs=out_specs, check_vma=False
    )
```

```python
import functools

import jax
import jax.numpy as jnp
from jax import lax
from jax.experimental import pallas as pl
from jax.experimental.pallas import tpu as pltpu
from jax.sharding import PartitionSpec as P

D = 4096
SHORT_LEN = 3
FILTER_LEN = 128
HALO = 144
Q = 256
CH = 256
F = 1024
epsilon = 1e-05
bf16 = jnp.bfloat16
f32 = jnp.float32


def ring(n, step):
    return [(i, (i + step) % n) for i in range(n)]


def shift(x, axis, step):
    return lax.ppermute(x, axis, ring(4, step))


TOKENS = 4 * Q


def project_kernel(quarters, row_ref, act_hbm, *refs):
    count = len(quarters)
    pieces, w_hbm, out_ref, x, w, scale_ref, x_sems, w_sems = refs[: 3 * count], *refs[3 * count :]
    row = row_ref[0]
    x_copies = []
    for s, quarter in enumerate(quarters):
        own = pl.ds(pl.multiple_of(lax.rem(row + quarter, 4) * Q, Q), Q)
        for b, source in enumerate([act_hbm.at[own, :], *pieces[3 * s : 3 * s + 3]]):
            x_copies.append(
                pltpu.make_async_copy(source, x.at[pl.ds(Q * s, Q), pl.ds(F * b, F)], x_sems.at[4 * s + b])
            )

    def w_copies(p):
        return [
            pltpu.make_async_copy(w_hbm.at[i, p], w.at[p, pl.ds(16 * i, 16), :], w_sems.at[p, i]) for i in range(16)
        ]

    for copy in x_copies + w_copies(0) + w_copies(1) + w_copies(2):
        copy.start()
    rows = 64
    for s in range(count):
        for copy in x_copies[4 * s : 4 * s + 4]:
            copy.wait()

        @pl.loop(Q * s // rows, Q * (s + 1) // rows)
        def _(i):
            at = pl.ds(pl.multiple_of(i * rows, rows), rows)
            squares = None
            for b in range(4):
                values = x[at, F * b : F * b + F].astype(f32)
                part = jnp.sum(values * values, axis=1, keepdims=True)
                squares = part if squares is None else squares + part
            scale_ref[at, :] = jnp.broadcast_to(lax.rsqrt(squares / D + epsilon), (rows, 128))

    @pl.loop(0, 3)
    def _(p):
        for copy in w_copies(p):
            copy.wait()
        total = lax.dot_general(x[...], w[p], (((1,), (1,)), ((), ())), preferred_element_type=f32)
        scale = scale_ref[...]
        for lanes in (slice(0, 128), slice(128, 256)):
            out_ref[p, :, lanes] = (total[:, lanes] * scale).astype(bf16)


def project(row, quarters, activations, pieces, w):
    count = len(quarters)
    anywhere = pl.BlockSpec(memory_space=pl.ANY)
    return pl.pallas_call(
        functools.partial(project_kernel, quarters),
        in_specs=[pl.BlockSpec(memory_space=pltpu.SMEM)] + [anywhere] * (3 * count + 2),
        out_specs=pl.BlockSpec(memory_space=pltpu.VMEM),
        out_shape=jax.ShapeDtypeStruct((3, count * Q, CH), bf16),
        scratch_shapes=[
            pltpu.VMEM((count * Q, D), bf16),
            pltpu.VMEM((3, CH, D), bf16),
            pltpu.VMEM((count * Q, 128), f32),
            pltpu.SemaphoreType.DMA((4 * count,)),
            pltpu.SemaphoreType.DMA((3, 16)),
        ],
        compiler_params=pltpu.CompilerParams(vmem_limit_bytes=56 << 20),
        cost_estimate=pl.CostEstimate(
            flops=4_000_000_000 * count, bytes_accessed=2 * (count * Q * D + 3 * CH * D), transcendentals=0
        ),
        name="project",
    )(row, activations, *pieces, w)


HALF = 512


def mix_kernel(first, row_ref, near_ref, far_ref, halo_ref, taps_ref, out_ref, qkv, gate, shifted):
    row = row_ref[0]
    if first:
        qkv[:, :HALO, :] = halo_ref[...].astype(f32)
    for s, (ref, at) in enumerate(((near_ref, 0), (near_ref, Q), (far_ref, 0), (near_ref, 2 * Q))):
        start = pl.multiple_of(lax.rem(row + s, 4) * Q + HALO, 16)
        for proj in range(3):
            qkv[proj, pl.ds(start, Q), :] = ref[proj, at : at + Q, :].astype(f32)
    offset = 0 if first else HALF

    step = 64

    @pl.loop(0, 2)
    def _(lane_block):
        lanes = pl.ds(pl.multiple_of(lane_block * 128, 128), 128)

        @pl.loop(0, (HALF + 128) // step)
        def _(i):
            base = pl.multiple_of(i * step, step) + (HALO - 128 + offset)
            total = []
            for proj in (1, 2):
                window = qkv[proj, pl.ds(pl.multiple_of(base - 8, 8), step + 8), lanes]
                acc = None
                for tap in range(SHORT_LEN):
                    term = taps_ref[pl.ds(3 * proj + tap, 1), lanes] * window[8 - tap : 8 - tap + step]
                    acc = term if acc is None else acc + term
                total.append(acc)
            gate[pl.ds(pl.multiple_of(i * step, step) + 8, step), lanes] = total[0] * total[1]

        @pl.loop(0, (HALF + 128) // 64)
        def _(i):
            base = pl.multiple_of(i * 64, 64)
            window = gate[pl.ds(base, 72), lanes]
            for r in range(8):
                shifted[r, pl.ds(base, 64), lanes] = window[8 - r : 72 - r]

        @pl.loop(0, HALF // 128)
        def _(i):
            base = pl.multiple_of(i * 128, 128)
            acc = taps_ref[pl.ds(137, 1), lanes] * gate[pl.ds(base + 136, 128), lanes]
            for r in range(8):
                window = shifted[r, pl.ds(base + 8, 248), lanes]
                for m in range(16):
                    acc = acc + taps_ref[pl.ds(9 + 8 * m + r, 1), lanes] * window[120 - 8 * m : 248 - 8 * m]
            window = qkv[0, pl.ds(base + (HALO - 8 + offset), 136), lanes]
            query = None
            for tap in range(SHORT_LEN):
                term = taps_ref[pl.ds(tap, 1), lanes] * window[8 - tap : 136 - tap]
                query = term if query is None else query + term
            out_ref[pl.ds(base, 128), lanes] = (query * acc).astype(bf16)


def mix(first, row, near, far, halo, taps):
    return pl.pallas_call(
        functools.partial(mix_kernel, first),
        in_specs=[pl.BlockSpec(memory_space=pltpu.SMEM)] + [pl.BlockSpec(memory_space=pltpu.VMEM)] * 4,
        out_specs=pl.BlockSpec(memory_space=pltpu.VMEM),
        out_shape=jax.ShapeDtypeStruct((HALF, CH), bf16),
        scratch_shapes=[
            pltpu.VMEM((3, HALO + 4 * Q, CH), f32),
            pltpu.VMEM((HALF + 136, CH), f32),
            pltpu.VMEM((8, HALF + 128, CH), f32),
        ],
        compiler_params=pltpu.CompilerParams(vmem_limit_bytes=24 << 20),
        cost_estimate=pl.CostEstimate(
            flops=9_000_000_000, bytes_accessed=2 << 20, transcendentals=0
        ),
        name="mix",
    )(row, near, far, halo, taps)


def shard_of(n):
    return n // 4 * 4 + n % 2 * 2 + n // 2 % 2


def after(x, *others):
    return lax.optimization_barrier((x, others))[0]


def gather_col(x):
    half = x.shape[0] // 2
    before = shift(x, "col", 1)
    behind = shift(x, "col", -1)
    far = [shift(before[:half], "col", 1), shift(behind[half:], "col", -1)]
    return [x, before, behind, jnp.concatenate(far, 0)]


HF = F // 2


def on_device(
    activations, norm_gain, w_query, w_key, w_value, short_taps, long_taps, skip_gain, w_out
):
    row = lax.axis_index("row")
    col = lax.axis_index("col")
    order = jnp.stack([col, (col + 3) % 4, (col + 1) % 4, (col + 2) % 4])

    stacked = (jnp.stack([w_query, w_key, w_value]).astype(f32) * norm_gain).astype(bf16).reshape(3, 4, 16, F)

    def group(i):
        return lax.dynamic_index_in_dim(stacked, i, 1, keepdims=False).reshape(48, F)

    own = lax.dynamic_slice_in_dim(activations, row * Q, Q, 0)

    def payload(x, w):
        return jnp.concatenate([x, w[:, :HF], w[:, HF:]], axis=0)

    up = shift(payload(own[:, :HF], group(order[2])), "col", 1)
    down = shift(payload(own[:, HF:], group(order[1])), "col", -1)
    w_far = shift(group(order[3]), "col", 2)
    w_rows = jnp.concatenate(
        [group(order[0]), up[Q : Q + 48], down[Q + 48 :], down[Q : Q + 48], up[Q + 48 :], w_far], axis=1
    )
    up, down = up[:Q], down[:Q]
    low_z = (lax.axis_index("ctx") // 2) % 2 == 0
    w_other = lax.ppermute(w_rows, "ctx", [(i, i ^ 2) for i in range(16)])
    w_pair = jnp.concatenate([jnp.where(low_z, w_rows, w_other), jnp.where(low_z, w_other, w_rows)], axis=0)
    mixed_up = jnp.concatenate([up, down], axis=1)
    up_from_before = shift(mixed_up, "row", 1)
    up_from_after = shift(mixed_up, "row", -1)
    rest = after(own, up, down)
    rest_up = shift(rest[:, HF:], "col", 1)
    rest_down = shift(rest[:, :HF], "col", -1)
    w_pair = after(w_pair, up_from_before, up_from_after, rest_up, rest_down)
    groups = [[4 * x + 2 * z + core for x in range(4) for core in range(2)] for z in range(2)]
    w_all = lax.all_gather(w_pair, "ctx", axis=0, tiled=True, axis_index_groups=groups).reshape(16, 3, 16, D)

    mixed_rest = jnp.concatenate([rest_down, rest_up], axis=1)
    up, down = after((up, down), rest_up, rest_down)
    far_up = shift(up, "col", 1)
    far_down = shift(down, "col", -1)
    from_before = [up_from_before, shift(mixed_rest, "row", 1)]
    from_after = [up_from_after, shift(mixed_rest, "row", -1)]
    mixed_far = after(jnp.concatenate([far_up, far_down], axis=1), from_before[1], from_after[1])
    from_before.append(shift(mixed_far, "row", 1))
    from_after.append(shift(mixed_far, "row", -1))
    own = [mixed_up, mixed_rest, mixed_far]
    far = [shift(from_before[0], "row", 1), shift(from_after[1], "row", -1)]
    far += [shift(from_before[2][:, :HF], "row", 1), shift(from_after[2][:, HF:], "row", -1)]
    near_out = project(row[None], (0, 1, 3), activations, own + from_after + from_before, w_all)
    small = jnp.concatenate(
        [short_taps.reshape(9, CH), long_taps, skip_gain[None], jnp.zeros((6, CH), f32)], axis=0
    )
    small = after(small, mixed_far)
    v = jnp.arange(512)
    wanted = shard_of(v % 128 // 16) * 64 + order[v // 128] * 16 + v % 16
    pick = ((jnp.arange(CH)[:, None] == wanted[None, :]) & (v % 128 < 64)[None, :]).astype(f32)
    small = jnp.dot(small, pick, precision=lax.Precision.HIGHEST)
    small = [
        small[:, :128],
        shift(small[:, 256:384], "col", 1),
        shift(small[:, 128:256], "col", -1),
        shift(small[:, 384:], "col", 2),
    ]
    far = after(far, near_out)
    far = far[:2] + [jnp.concatenate(far[2:], axis=1)]
    far_out = project(row[None], (2,), activations, far, w_all)

    small = after(small, near_out)
    place = ((order[v // 128] * 64 + v % 128)[:, None] == jnp.arange(CH)[None, :]) & (v % 128 < 64)[:, None]
    taps = jnp.dot(jnp.concatenate(small, axis=1), place.astype(f32), precision=lax.Precision.HIGHEST)

    m = jnp.arange(F)
    blocks = order[m // 256]
    wanted_out = shard_of((m % 256) // 16) * 64 + blocks * 16 + m % 16
    pick_out = (jnp.arange(F)[:, None] == wanted_out[None, :]).astype(bf16)
    w_out = after(w_out, from_before[2])
    out_rows = jnp.dot(w_out, pick_out, preferred_element_type=f32).astype(bf16)
    out_all = lax.all_gather(out_rows, "ctx", axis=0, tiled=True)

    tails = [near_out[:, Q - HALO : Q], near_out[:, 2 * Q - HALO : 2 * Q], far_out[:, Q - HALO :], near_out[:, 3 * Q - HALO :]]
    tail = lax.dynamic_index_in_dim(jnp.stack(tails), (3 - row) % 4, 0, keepdims=False)
    halo = lax.ppermute(tail, "ctx", [(i, i + 1) for i in range(15)])

    late = mix(False, row[None], near_out, far_out, tail, taps)
    early = mix(True, row[None], near_out, far_out, halo, taps)
    mixed = jnp.concatenate([early, late], axis=0).reshape(4, Q, CH)

    def quarter(s):
        return lax.dynamic_index_in_dim(mixed, (row + s) % 4, 0, keepdims=False)

    mid = Q // 2
    opposite, above, below = quarter(2), quarter(1), quarter(3)
    first = gather_col(jnp.concatenate([opposite, above[:mid], below[mid:]], axis=0))
    second = jnp.concatenate([above[mid:], below[:mid], quarter(0)], axis=0)
    second = gather_col(second)

    def outputs(gathered):
        return lax.dot_general(
            jnp.concatenate(gathered, axis=1), out_all, (((1,), (1,)), ((), ())), preferred_element_type=f32
        ).astype(bf16)

    def add(a, b):
        return (a.astype(f32) + b.astype(f32)).astype(bf16)

    part = outputs(first)
    opposite_lo = shift(part[:mid], "row", 1)
    opposite_hi = shift(part[mid:Q], "row", -1)
    up_lo = shift(add(part[Q : Q + mid], opposite_lo), "row", 1)
    down_hi = shift(add(part[Q + mid :], opposite_hi), "row", -1)
    part = outputs(second)
    up_hi = shift(part[:mid], "row", 1)
    down_lo = shift(part[mid:Q], "row", -1)
    up = jnp.concatenate([up_lo, up_hi], axis=0)
    down = jnp.concatenate([down_lo, down_hi], axis=0)
    return (part[Q:].astype(f32) + up.astype(f32) + down.astype(f32)).astype(bf16)


def solution(mesh):
    in_specs = (
        P("ctx", "col"),
        P("col"),
        P(("row", "ctx"), "col"),
        P(("row", "ctx"), "col"),
        P(("row", "ctx"), "col"),
        P(None, None, ("row", "col")),
        P(None, ("row", "col")),
        P(("row", "col")),
        P(("col", "ctx"), "row"),
    )
    out_specs = P(("ctx", "row"), "col")
    return jax.shard_map(
        on_device, mesh=mesh, in_specs=in_specs, out_specs=out_specs, check_vma=False
    )
```
